32 devices in a mesh: grp: 2 (over y), epoch: 4 (over x, core), asset: 4 (over z).
Axes of the slice: x: 2, y: 2, z: 4, core: 2. Of those that a mesh axis runs over, the one named last changes fastest.
Arguments:
- signals: bfloat16 [8, 1024, 256], P(('grp', 'epoch'), 'asset'), parts along dimension 0, may hold values from -6 to 6
- targets: bfloat16 [8, 1024, 256], P(('grp', 'epoch'), 'asset'), parts along dimension 0, may hold values from -6 to 6
- row_counts: int32 [8, 4], P(('grp', 'epoch'), 'asset'), parts along dimension 0, may hold values from 32 to 256, as said below
- feature_weights: bfloat16 [256, 2048], replicated, may hold values from -0.375 to 0.375
- phases: float32 [2048], replicated, may hold values from -3.140625 to 3.140625
- spread_ids: int32 [2048], replicated, may hold values from 0 to 3
Outputs:
- coefficients: float32 [8, 2048, 256], P(('grp', 'epoch'), 'asset'), parts along dimension 0
The draws below stay inside these ranges and needn't reach their ends.
There are 2 independent parts, one for each index of `grp`. The reference program is written for one: setup_inputs(seed, part) draws one part's arguments, and reference() takes and returns one part's arrays. A program takes and returns all parts, laid end to end along the dimension named above; an argument that names none is the same for every part. Nothing has to cross between parts.
Inputs may be any that keep to these rules, and one draw needn't show every extreme that they name: `row_counts`: each count is at least 32, and in every epoch some asset group has exactly 256 live rows.
All inputs are finite; a program needn't handle non-finite values.
Results may differ from the reference program's by a relative error of at most 0.0003.
Values may be sent and summed in bfloat16 or wider, within the bound.
No kernel may reach another device: no remote copies, remote signals or barrier semaphores. Data moves between devices by JAX's collectives and lax.ppermute only.
A program may use at most 64 MiB of HBM per device.

```python
import jax
import jax.numpy as jnp
from jax import lax

F = 2048
TGT = 256
K = 256
R_DEV = 256
ITERS = 3
EPOCHS = 4
ASSETS = 4


def shared_factors(key):
    sign_key, load_key, target_key = jax.random.split(jax.random.fold_in(key, 23), 3)
    sign_bits = jax.random.randint(sign_key, (EPOCHS, ASSETS * R_DEV, 4), 0, 2)
    factor_signs = (2 * sign_bits - 1).astype(jnp.float32)
    loadings = jax.random.normal(load_key, (4, K), jnp.float32)
    target_loads = jax.random.normal(target_key, (4, TGT), jnp.float32)
    return (factor_signs, loadings, target_loads)


def draw_signals(key, part):
    factor_signs, loadings, target_loads = shared_factors(key)
    noise_key = jax.random.fold_in(key, 29)
    base_noise = jax.random.normal(noise_key, (EPOCHS, ASSETS * R_DEV, K), jnp.float32)
    strengths = (0.6, 0.8, 1.0, 1.2)
    values = base_noise
    for factor in range(4):
        values = values + strengths[factor] * factor_signs[:, :, factor:factor + 1] * loadings[factor][None, None, :]
    return jnp.clip(values, -6.0, 6.0).astype(jnp.bfloat16)


def draw_targets(key, part):
    factor_signs, loadings, target_loads = shared_factors(key)
    noise_key = jax.random.fold_in(key, 31)
    base_noise = jax.random.normal(noise_key, (EPOCHS, ASSETS * R_DEV, TGT), jnp.float32)
    strengths = (0.5, 0.6, 0.7, 0.8)
    values = base_noise
    for factor in range(4):
        values = values + strengths[factor] * factor_signs[:, :, factor:factor + 1] * target_loads[factor][None, None, :]
    return jnp.clip(values, -6.0, 6.0).astype(jnp.bfloat16)


def draw_row_counts(key, part):
    first_key, second_key = jax.random.split(jax.random.fold_in(key, 11))
    lowest = R_DEV // 8
    levels = jax.random.randint(first_key, (EPOCHS, ASSETS), 0, 1001)
    counts = lowest + (R_DEV - lowest) * (levels * levels // 1000) // 1000
    chosen = jax.random.randint(second_key, (EPOCHS, 1), 0, ASSETS)
    counts = jnp.where(jnp.arange(ASSETS)[None, :] == chosen, R_DEV, counts)
    return counts.astype(jnp.int32)


def plant(values, own_key, least, high):
    longest = values.shape.index(max(values.shape))
    spots = []
    for shift in (0, 1):
        where = [jax.random.randint(jax.random.fold_in(own_key, axis), (), 0, length) for axis, length in enumerate(values.shape)]
        where[longest] = (where[longest] + shift) % values.shape[longest]
        spots.append(tuple(where))
    return values.at[spots[0]].set(least).at[spots[1]].set(high)


def noise(own_key, dims, width, reach, held_as=jnp.bfloat16):
    result = jax.random.normal(own_key, dims, jnp.float32) * width
    return jnp.minimum(jnp.maximum(result, -reach), reach).astype(held_as)


def setup_inputs(seed: int = 0, part: int = 0) -> dict:
    key_of = jax.random.split(jax.random.key(seed), 7)
    part_splits = jax.random.split(jax.random.fold_in(key_of[6], part), 7)
    return {
        "signals": draw_signals(jax.random.fold_in(jax.random.fold_in(key_of[6], part), 71), part),
        "targets": draw_targets(jax.random.fold_in(jax.random.fold_in(key_of[6], part), 71), part),
        "row_counts": draw_row_counts(jax.random.fold_in(jax.random.fold_in(key_of[6], part), 71), part),
        "feature_weights": noise(key_of[3], (K, F), K ** -0.5, 0.375),
        "phases": jnp.clip(jax.random.uniform(key_of[4], (F,), jnp.float32, -3.140625, 3.140625), -3.140625, 3.140625),
        "spread_ids": plant(jax.random.randint(key_of[5], (F,), 0, 4), jax.random.fold_in(key_of[5], 1), 0, 3).astype(jnp.int32),
    }


ridge_penalty = 0.05
epsilon = 1e-06

def feature_scale(spread_ids):
    return (0.5 * (1.0 + jnp.where(spread_ids >= 1, 1.0, 0.0) + jnp.where(spread_ids >= 2, 2.0, 0.0) + jnp.where(spread_ids >= 3, 4.0, 0.0))).astype(jnp.float32)

def make_features(inputs, feature_weights, phases, spread_ids):
    projected = jnp.dot(inputs, feature_weights, preferred_element_type=jnp.float32)
    return jnp.sin(projected * feature_scale(spread_ids) + phases).astype(jnp.float32)

def reference(signals, targets, row_counts, feature_weights, phases, spread_ids):
    entries = F * TGT
    slot_index = jnp.arange(ASSETS * R_DEV) % R_DEV
    owner = jnp.arange(ASSETS * R_DEV) // R_DEV
    identity = jnp.eye(F, dtype=jnp.float32)

    def advance(state, inputs):
        summed, row_total = state
        rows_in, returns, counts = inputs
        features = make_features(rows_in, feature_weights, phases, spread_ids)
        live_mask = (slot_index < counts[owner])[:, None]
        features = jnp.where(live_mask, features, jnp.zeros_like(features))
        returns = jnp.where(live_mask, returns.astype(jnp.float32), jnp.zeros((), jnp.float32))
        combined = jnp.concatenate([features, returns], axis=1)
        group_features = features.reshape(ASSETS, R_DEV, F)
        group_combined = combined.reshape(ASSETS, R_DEV, F + TGT)

        def add_group(running, pieces):
            piece_features, piece_combined = pieces
            term = jnp.dot(piece_features.T, piece_combined, precision=lax.Precision.HIGHEST)
            return (running + term, None)
        epoch_terms, unused = lax.scan(add_group, jnp.zeros((F, F + TGT), jnp.float32), (group_features, group_combined))
        summed = summed + epoch_terms
        row_total = row_total + jnp.sum(counts).astype(jnp.float32)
        system = summed[:, :F] / row_total + ridge_penalty * identity
        residual = summed[:, F:] / row_total
        coef = jnp.zeros((F, TGT), jnp.float32)
        for iteration in range(ITERS):
            image = jnp.dot(system, residual, precision=lax.Precision.HIGHEST)
            res_norm = jnp.sum(residual * residual)
            res_curve = jnp.sum(residual * image)
            step_size = res_norm / entries / (res_curve / entries + epsilon)
            coef = coef + step_size * residual
            residual = residual - step_size * image
        return ((summed, row_total), jnp.sqrt(row_total) * coef)
    start_state = (jnp.zeros((F, F + TGT), jnp.float32), jnp.zeros((), jnp.float32))
    final_state, coefficients = lax.scan(advance, start_state, (signals, targets, row_counts))
    return coefficients
```

```python
import jax
import jax.numpy as jnp
from jax import lax
from jax.experimental import pallas as pl
from jax.experimental.pallas import tpu as pltpu
from jax.sharding import PartitionSpec as P

ITERS = 3


ridge_penalty = 0.05
epsilon = 1e-06

CHUNK = 256
TILE = 256
PACK = 16
SHARED = 8
SUBLANES = 16
LANES = 128
TURN = 0.15915494309189535
SINE = (
    6.283182818537488,
    -41.34142139758713,
    81.59618384799899,
    -76.58010029406394,
    41.20539392705353,
    -12.27126097383172,
)
NT = (((1,), (1,)), ((), ()))
NN = (((1,), (0,)), ((), ()))


def prefix(part, axis, combine, identity):
    place = lax.axis_index(axis)
    gathered = jax.tree.map(lambda a: lax.all_gather(a, axis), part)
    state = jax.tree.map(lambda a, e: jnp.zeros_like(a) + jnp.asarray(e, a.dtype), part, identity)

    def one(hop, state):
        return combine(
            state, jax.tree.map(lambda a: lax.dynamic_index_in_dim(a, hop, 0, False), gathered)
        )

    return lax.fori_loop(0, place, one, state)


def feature_scale(spread_ids):
    return (
        0.5
        * (
            1.0
            + jnp.where(spread_ids >= 1, 1.0, 0.0)
            + jnp.where(spread_ids >= 2, 2.0, 0.0)
            + jnp.where(spread_ids >= 3, 4.0, 0.0)
        )
    ).astype(jnp.float32)


def make_features(inputs, feature_weights, phases, spread_ids):
    projected = jnp.dot(inputs, feature_weights, preferred_element_type=jnp.float32)
    return jnp.sin(projected * feature_scale(spread_ids) + phases)


def add_pair(earlier, later):
    return (earlier[0] + later[0], earlier[1] + later[1])


def gram_form(signals, targets, row_counts, feature_weights, phases, spread_ids):
    rows = signals.shape[1]
    width = feature_weights.shape[1]
    tgt_width = targets.shape[2]
    groups = lax.axis_size("asset")
    block_size = width // groups
    entries = width * tgt_width
    own_rows = row_counts[0, 0]
    all_counts = lax.all_gather(row_counts[0], "asset", axis=0, tiled=True)
    row_sum = jnp.sum(all_counts).astype(jnp.float32)
    inputs = signals[0]
    returns = targets[0]
    features = make_features(inputs, feature_weights, phases, spread_ids)
    live_mask = (jnp.arange(rows) < own_rows)[:, None]
    features = jnp.where(live_mask, features, jnp.zeros_like(features))
    returns = jnp.where(live_mask, returns.astype(jnp.float32), jnp.zeros((), jnp.float32))
    combined = jnp.concatenate([features, returns], axis=1)
    contract_rows = (((0,), (0,)), ((), ()))
    gram_block = lax.psum_scatter(
        lax.dot_general(features, combined, contract_rows, precision=lax.Precision.HIGHEST),
        "asset",
        scatter_dimension=0,
        tiled=True,
    )
    earlier, earlier_rows = prefix(
        (gram_block, row_sum),
        "epoch",
        add_pair,
        (jnp.zeros_like(gram_block), jnp.zeros((), jnp.float32)),
    )
    cumulative = earlier + gram_block
    row_total = earlier_rows + row_sum
    first_row = lax.axis_index("asset") * block_size
    diagonal = jnp.arange(width)[None, :] == first_row + jnp.arange(block_size)[:, None]
    system = cumulative[:, :width] / row_total + ridge_penalty * jnp.where(
        diagonal, 1.0, 0.0
    ).astype(jnp.float32)
    residual = cumulative[:, width:] / row_total
    coef = jnp.zeros((block_size, tgt_width), jnp.float32)
    for iteration in range(ITERS):
        image = jnp.zeros((block_size, tgt_width), jnp.float32) + jnp.dot(
            system,
            lax.all_gather(residual, "asset", axis=0, tiled=True),
            precision=lax.Precision.HIGHEST,
        )
        res_norm, res_curve = lax.psum(
            (jnp.sum(residual * residual), jnp.sum(residual * image)), "asset"
        )
        step_size = res_norm / entries / (res_curve / entries + epsilon)
        coef = coef + step_size * residual
        residual = residual - step_size * image
    return (jnp.sqrt(row_total) * coef)[None]


def dot(a, b, dims):
    return lax.dot_general(a, b, dims, preferred_element_type=jnp.float32)


def split(a):
    high = a.astype(jnp.bfloat16)
    return high, (a - high.astype(jnp.float32)).astype(jnp.bfloat16)


def sine_of_turns(turns):
    fraction = turns - jnp.round(turns)
    square = fraction * fraction
    value = SINE[-1]
    for c in SINE[-2::-1]:
        value = value * square + c
    return value * fraction


def kernel_call(kernel, out_shape, in_specs, out_specs, scratch, cost=None):
    return pl.pallas_call(
        kernel,
        out_shape=out_shape,
        in_specs=in_specs,
        out_specs=out_specs,
        scratch_shapes=scratch,
        cost_estimate=cost,
        compiler_params=pltpu.CompilerParams(vmem_limit_bytes=60 * 2**20),
    )


WHOLE = pl.BlockSpec(memory_space=pltpu.VMEM)
SCALARS = pl.BlockSpec(memory_space=pltpu.SMEM)
REMOTE = pl.BlockSpec(memory_space=pl.ANY)


def rows_of(c):
    return pl.ds(pl.multiple_of(c * CHUNK, CHUNK), CHUNK)


def pack_rows(sources, rows, mark, x_buf, y_buf):
    lane = lax.broadcasted_iota(jnp.int32, (1, LANES), 1)
    counts = []
    for x_ref, y_ref, use in sources:
        for first in range(0, x_ref.shape[0], rows):
            marks = jnp.sum(y_ref[first : first + rows, :].astype(jnp.float32), axis=0, keepdims=True)
            counts.append(jnp.sum(jnp.where(lane == mark, marks, 0.0)).astype(jnp.int32) * use)
    filled = jnp.int32(0)
    count = jnp.int32(0)
    place = 0
    for x_ref, y_ref, use in sources:
        for first in range(0, x_ref.shape[0], rows):
            own = counts[place]
            place += 1
            at = pl.ds(pl.multiple_of(filled, PACK), rows)
            x_buf[at, :] = x_ref[first : first + rows, :]
            y_buf[at, :] = y_ref[first : first + rows, :]
            count = count + own
            filled = filled + (own + PACK - 1) // PACK * PACK
    end = pl.ds(pl.multiple_of(filled, PACK), CHUNK)
    x_buf[end, :] = jnp.zeros((CHUNK, x_buf.shape[1]), x_buf.dtype)
    y_buf[end, :] = jnp.zeros((CHUNK, LANES), y_buf.dtype)
    return (filled + CHUNK - 1) // CHUNK, count


def featurize_chunk(x, y, lines, w_ref, ph_ref, cross_ref, put):
    returns = y[:lines].astype(jnp.bfloat16)
    for j in range(0, w_ref.shape[1], TILE):
        js = slice(j, j + TILE)
        turns = dot(x, w_ref[:, js], NN) * TURN + ph_ref[:, js]
        high, low = split(sine_of_turns(turns))
        put(js, high, low)
        cross_ref[:, js] += dot(returns, high, NN) + dot(returns, low, NN)


def near_kernel(sources, rows, lines, mark, use_ref, *refs):
    x_refs, y_refs = refs[:sources], refs[sources : 2 * sources]
    w_ref, ph_ref, high_hbm, low_hbm, cross_ref, live_ref, info_ref = refs[2 * sources : 2 * sources + 7]
    x_buf, y_buf, high_buf, low_buf, high_sem, low_sem = refs[2 * sources + 7 :]
    sets = [(x_refs[s], y_refs[s], use_ref[s]) for s in range(sources)]
    chunks, count = pack_rows(sets, rows, mark, x_buf, y_buf)
    info_ref[0] = chunks
    info_ref[1] = count
    cross_ref[...] = jnp.zeros_like(cross_ref)

    def send(c, slot):
        return (
            pltpu.make_async_copy(high_buf.at[slot], high_hbm.at[rows_of(c), :], high_sem.at[slot]),
            pltpu.make_async_copy(low_buf.at[slot], low_hbm.at[rows_of(c), :], low_sem.at[slot]),
        )

    def one(c, _):
        slot = lax.rem(c, 2)

        @pl.when(c >= 2)
        def _():
            for copy in send(c - 2, slot):
                copy.wait()

        turned = y_buf[rows_of(c), :].astype(jnp.float32).T
        live_ref[c] = turned[mark : mark + 8]

        def put(js, high, low):
            high_buf[slot, :, js] = high
            low_buf[slot, :, js] = low

        featurize_chunk(x_buf[rows_of(c), :], turned, lines, w_ref, ph_ref, cross_ref, put)
        for copy in send(c, slot):
            copy.start()
        return 0

    lax.fori_loop(0, chunks, one, 0)
    for back in (2, 1):

        @pl.when(chunks >= back)
        def _():
            for copy in send(chunks - back, lax.rem(chunks - back, 2)):
                copy.wait()


def estimate(cols, r, i):
    f32 = jnp.float32
    norm = jnp.full((1, 1), jnp.sum(r[cols : cols + SHARED] * r[cols : cols + SHARED]), f32)
    curve = jnp.full((1, 1), jnp.sum(r[cols : cols + SHARED] * i[cols : cols + SHARED]), f32)
    good = jnp.logical_and(norm > 0.0, curve > ridge_penalty * 0.5 * norm)
    return jnp.where(good, norm / jnp.where(good, curve, 1.0), 1.0)


def main_kernel(sources, rows, lines, cols, mark, use_ref, info_ref, *refs):
    x_refs, y_refs = refs[:sources], refs[sources : 2 * sources]
    w_ref, ph_ref, near_cross, near_live, near_high, near_low = refs[2 * sources : 2 * sources + 6]
    v0_ref, q1_ref, q2_ref, mom_ref = refs[2 * sources + 6 : 2 * sources + 10]
    x_buf, y_buf, phi, plo, live, stack, inner, acc, v0, image, q1, high_sem, low_sem = refs[2 * sources + 10 :]
    f32, bf16 = jnp.float32, jnp.bfloat16

    near = info_ref[0]

    def begin(c, _):
        at = rows_of(c)
        pltpu.make_async_copy(near_high.at[at, :], phi.at[at, :], high_sem.at[c]).start()
        pltpu.make_async_copy(near_low.at[at, :], plo.at[at, :], low_sem.at[c]).start()
        live[c] = near_live[c]
        return 0

    lax.fori_loop(0, near, begin, 0)
    sets = [(x_refs[s], y_refs[s], use_ref[s]) for s in range(sources)]
    far, count = pack_rows(sets, rows, mark, x_buf, y_buf)
    chunks = near + far
    total = (info_ref[1] + count).astype(f32)
    inverse = 1.0 / jnp.full((1, 1), total, f32)

    v0[...] = near_cross[...]

    def featurize(c, _):
        turned = y_buf[rows_of(c), :].astype(f32).T
        live[near + c] = turned[mark : mark + 8]
        at = rows_of(near + c)

        def put(js, high, low):
            phi[at, js] = high
            plo[at, js] = low

        featurize_chunk(x_buf[rows_of(c), :], turned, lines, w_ref, ph_ref, v0, put)
        return 0

    lax.fori_loop(0, far, featurize, 0)

    def end(c, _):
        at = rows_of(c)
        pltpu.make_async_copy(near_high.at[at, :], phi.at[at, :], high_sem.at[c]).wait()
        pltpu.make_async_copy(near_low.at[at, :], plo.at[at, :], low_sem.at[c]).wait()
        return 0

    lax.fori_loop(0, near, end, 0)
    v0[...] = v0[...] * inverse

    high, low = split(v0[...])
    stack[:lines] = high
    stack[lines:] = low
    acc[...] = jnp.zeros_like(acc)

    def inner_first(c):
        u = dot(stack[...], phi[rows_of(c), :], NT)
        uh, ul = split((u[:lines] + u[lines:]) * live[c][0:1])
        inner[lax.rem(c, 2), :lines] = uh
        inner[lax.rem(c, 2), lines:] = ul

    def first(c, _):
        slot = lax.rem(c, 2)
        held = inner[slot]
        acc[...] += dot(held, phi[rows_of(c), :], NN)
        acc[:lines] += dot(held[:lines], plo[rows_of(c), :], NN)
        inner_first(jnp.minimum(c + 1, chunks - 1))
        return 0

    inner_first(0)
    lax.fori_loop(0, chunks, first, 0)
    image[...] = (acc[:lines] + acc[lines:]) * inverse + ridge_penalty * v0[...]
    shift0 = estimate(cols, v0, image)
    q1[...] = v0[...] - shift0 * image[...]
    stack[:lines] = q1[...].astype(bf16)
    acc[:lines] = jnp.zeros((lines, acc.shape[1]), f32)

    def inner_second(c):
        u = dot(stack[:lines], phi[rows_of(c), :], NT) * live[c][0:1]
        inner[lax.rem(c, 2), :lines] = u.astype(bf16)

    def second(c, _):
        held = inner[lax.rem(c, 2), :lines]
        acc[:lines] += dot(held, phi[rows_of(c), :], NN)
        inner_second(jnp.minimum(c + 1, chunks - 1))
        return 0

    inner_second(0)
    lax.fori_loop(0, chunks, second, 0)
    acc[:lines] = acc[:lines] * inverse + ridge_penalty * q1[...]
    shift1 = estimate(cols, q1, acc)
    v0_ref[...] = v0[:cols]
    q1_ref[...] = q1[:cols]
    q2_ref[...] = q1[:cols] - shift1 * acc[:cols]
    stack[:cols] = q2_ref[...].astype(bf16)

    def curve(c, total_sq):
        u = dot(stack[:cols], phi[rows_of(c), :], NT) * live[c][0:1]
        return total_sq + u * u

    squares = lax.fori_loop(0, chunks, curve, jnp.zeros((cols, CHUNK), f32))
    vectors = (v0_ref, q1_ref, q2_ref)
    images = (image, acc)
    pairs = [jnp.sum(vectors[i][...] * vectors[j][...]) for i in range(3) for j in range(i, 3)]
    pairs += [jnp.sum(vectors[i][...] * images[j][:cols]) for j in range(2) for i in range(j, 3)]
    pairs.append(jnp.sum(squares) / total + ridge_penalty * pairs[5])
    for i, m in enumerate(pairs):
        mom_ref[i] = m
    mom_ref[12] = jnp.sum(shift0)
    mom_ref[13] = jnp.sum(shift1)
    mom_ref[14] = total
    mom_ref[15] = total


def finish_kernel(groups, entries, sum_ref, mom_ref, v0_ref, q1_ref, q2_ref, out_ref):
    f32 = jnp.float32

    def row(ref, i):
        return jnp.full((1, LANES), ref[i], f32)

    g = {}
    for n, (i, j) in enumerate(((0, 0), (0, 1), (0, 2), (1, 1), (1, 2), (2, 2))):
        g[i, j] = g[j, i] = row(sum_ref, n) / entries
    h = {}
    for n, (i, j) in enumerate(((0, 0), (1, 0), (2, 0), (1, 1), (2, 1), (2, 2))):
        h[i, j] = h[j, i] = row(sum_ref, 6 + n) / entries
    shift0, shift1, total = row(mom_ref, 12), row(mom_ref, 13), row(mom_ref, 14)

    def form(table, r):
        return sum(r[i] * r[j] * table[i, j] for i in range(3) for j in range(3))

    def step_of(r):
        return jnp.clip(form(g, r) / (form(h, r) + epsilon), 0.0, 1.0 / ridge_penalty)

    one = jnp.ones((1, LANES), f32)
    zero = jnp.zeros((1, LANES), f32)
    r0 = (one, zero, zero)
    step0 = g[0, 0] / (h[0, 0] + epsilon)
    ratio = step0 / shift0
    r1 = (one - ratio, ratio, zero)
    step1 = step_of(r1)
    left, right = r1[0] / shift0, r1[1] / shift1
    r2 = (r1[0] - step1 * left, r1[1] - step1 * (right - left), step1 * right)
    step2 = step_of(r2)
    root = jnp.sqrt(total)
    k = [(root * (step0 * r0[i] + step1 * r1[i] + step2 * r2[i]))[:, :1] for i in range(3)]
    piece = v0_ref.shape[1] // groups
    for owner in range(groups):
        at = slice(owner * piece, (owner + 1) * piece)
        out_ref[owner] = k[0] * v0_ref[:, at] + k[1] * q1_ref[:, at] + k[2] * q2_ref[:, at]


def factor_form(signals, targets, row_counts, feature_weights, phases, spread_ids):
    _, rows, depth = signals.shape
    width = feature_weights.shape[1]
    tgt_width = targets.shape[2]
    groups = lax.axis_size("asset")
    epochs = lax.axis_size("epoch")
    cols = tgt_width // groups
    mark = cols + SHARED
    lines = (mark + 1 + SUBLANES - 1) // SUBLANES * SUBLANES
    piece = width // groups
    f32, bf16 = jnp.float32, jnp.bfloat16
    asset = lax.axis_index("asset")
    epoch = lax.axis_index("epoch")

    def rotate(a, s):
        return lax.ppermute(a, "asset", [(i, (i + s) % groups) for i in range(groups)])

    def swap(a, bit):
        return lax.ppermute(a, "epoch", [(e, e ^ bit) for e in range(epochs)])

    x = signals[0]
    x_own = [x] + [rotate(x, s) for s in range(1, groups)]
    alive = (jnp.arange(rows) < row_counts[0, 0])[:, None]
    returns = jnp.where(alive, targets[0], jnp.zeros((), bf16))
    rest = jnp.concatenate(
        [returns[:, :SHARED], alive.astype(bf16), jnp.zeros((rows, LANES - mark - 1), bf16)], axis=1
    )
    payload = jnp.stack(
        [
            jnp.concatenate([returns[:, g * cols : (g + 1) * cols], rest], axis=1)
            for g in range(groups)
        ]
    )
    y_own = []
    for s in range(groups):
        mine = lax.dynamic_index_in_dim(payload, (asset + s) % groups, 0, False)
        y_own.append(rotate(mine, s) if s else mine)
    y_own = jnp.concatenate(y_own)
    held = [(x_own, y_own, 0)]
    bit = epochs // 2
    while bit > 1:
        held = held + [([swap(b, bit) for b in xs], swap(y, bit), o ^ bit) for xs, y, o in held]
        bit //= 2
    held = [(jnp.concatenate(xs), y, o) for xs, y, o in held]
    held = held + [(swap(xs, 1), swap(y, 1), o ^ 1) for xs, y, o in held]
    near = [h for h in held if h[2] < 2]
    far = [h for h in held if h[2] >= 2]

    def used(sources):
        return jnp.stack([((epoch ^ o) <= epoch).astype(jnp.int32) for _, _, o in sources])

    scaled = (feature_weights.astype(f32) * feature_scale(spread_ids)).astype(bf16)
    offsets = (phases * TURN)[None, :]

    def shape(*dims, dtype=f32):
        return jax.ShapeDtypeStruct(dims, dtype)

    span = groups * rows
    limit = len(near) * span
    high, low, cross, live, info = kernel_call(
        lambda *refs: near_kernel(len(near), rows, lines, mark, *refs),
        (
            shape(limit, width, dtype=bf16),
            shape(limit, width, dtype=bf16),
            shape(lines, width),
            shape(limit // CHUNK, 8, CHUNK),
            shape(2, dtype=jnp.int32),
        ),
        [SCALARS] + [WHOLE] * (2 * len(near) + 2),
        (REMOTE, REMOTE, WHOLE, WHOLE, SCALARS),
        [
            pltpu.VMEM((limit + CHUNK, depth), bf16),
            pltpu.VMEM((limit + CHUNK, LANES), bf16),
            pltpu.VMEM((2, CHUNK, width), bf16),
            pltpu.VMEM((2, CHUNK, width), bf16),
            pltpu.SemaphoreType.DMA((2,)),
            pltpu.SemaphoreType.DMA((2,)),
        ],
        pl.CostEstimate(flops=10**10, transcendentals=limit * width, bytes_accessed=5 * 10**7),
    )(used(near), *[a for a, _, _ in near], *[y for _, y, _ in near], scaled, offsets)

    limit = len(far) * span
    whole = len(held) * span
    vector = shape(cols, width)
    v0, q1, q2, moments = kernel_call(
        lambda *refs: main_kernel(len(far), rows, lines, cols, mark, *refs),
        (vector, vector, vector, shape(16)),
        [SCALARS] * 2 + [WHOLE] * (2 * len(far) + 4) + [REMOTE] * 2,
        (WHOLE, WHOLE, WHOLE, SCALARS),
        [
            pltpu.VMEM((limit + CHUNK, depth), bf16),
            pltpu.VMEM((limit + CHUNK, LANES), bf16),
            pltpu.VMEM((whole, width), bf16),
            pltpu.VMEM((whole, width), bf16),
            pltpu.VMEM((whole // CHUNK, 8, CHUNK), f32),
            pltpu.VMEM((2 * lines, width), bf16),
            pltpu.VMEM((2, 2 * lines, CHUNK), bf16),
            pltpu.VMEM((2 * lines, width), f32),
            pltpu.VMEM((lines, width), f32),
            pltpu.VMEM((lines, width), f32),
            pltpu.VMEM((lines, width), f32),
            pltpu.SemaphoreType.DMA((len(near) * span // CHUNK,)),
            pltpu.SemaphoreType.DMA((len(near) * span // CHUNK,)),
        ],
    )(
        used(far), info, *[a for a, _, _ in far], *[y for _, y, _ in far],
        scaled, offsets, cross, live, high, low,
    )
    sums = lax.psum(moments, "asset")
    coef = kernel_call(
        lambda *refs: finish_kernel(groups, width * tgt_width, *refs),
        shape(groups, cols, piece),
        [SCALARS] * 2 + [WHOLE] * 3,
        WHOLE,
        [],
    )(sums, moments, v0, q1, q2)
    coef = lax.all_to_all(coef, "asset", 0, 0, tiled=True)
    return coef.reshape(tgt_width, piece).T[None]


def on_device(signals, targets, row_counts, feature_weights, phases, spread_ids):
    epochs = lax.axis_size("epoch")
    groups = lax.axis_size("asset")
    width = feature_weights.shape[1]
    rows = signals.shape[1]
    cols = targets.shape[2] // groups
    fits = (
        epochs * groups * rows <= 2 * width
        and epochs & (epochs - 1) == 0
        and epochs >= 4
        and rows % CHUNK == 0
        and width % TILE == 0
        and cols % 8 == 0
        and (width // groups) % LANES == 0
        and cols + SHARED + 8 <= LANES
    )
    form = factor_form if fits else gram_form
    return form(signals, targets, row_counts, feature_weights, phases, spread_ids)


def solution(mesh):
    placed = (
        P(("grp", "epoch"), "asset", None),
        P(("grp", "epoch"), "asset", None),
        P(("grp", "epoch"), "asset"),
        P(),
        P(),
        P(),
    )
    return jax.shard_map(
        on_device,
        mesh=mesh,
        in_specs=placed,
        out_specs=P(("grp", "epoch"), "asset", None),
        check_vma=False,
    )
```

```python
import jax
import jax.numpy as jnp
from jax import lax
from jax.experimental import pallas as pl
from jax.experimental.pallas import tpu as pltpu
from jax.sharding import PartitionSpec as P


ITERS = 3


ridge_penalty = 0.05
epsilon = 1e-06

CHUNK = 256
GROUP = 4
TILE = 256
PACK = 16
SHARED = 8
SUBLANES = 16
LANES = 128
TURN = 0.15915494309189535
SINE = (
    6.283182818537488,
    -41.34142139758713,
    81.59618384799899,
    -76.58010029406394,
    41.20539392705353,
    -12.27126097383172,
)
NT = (((1,), (1,)), ((), ()))
NN = (((1,), (0,)), ((), ()))


def prefix(part, axis, combine, identity):
    place = lax.axis_index(axis)
    gathered = jax.tree.map(lambda a: lax.all_gather(a, axis), part)
    state = jax.tree.map(lambda a, e: jnp.zeros_like(a) + jnp.asarray(e, a.dtype), part, identity)

    def one(hop, state):
        return combine(
            state, jax.tree.map(lambda a: lax.dynamic_index_in_dim(a, hop, 0, False), gathered)
        )

    return lax.fori_loop(0, place, one, state)


def feature_scale(spread_ids):
    return (
        0.5
        * (
            1.0
            + jnp.where(spread_ids >= 1, 1.0, 0.0)
            + jnp.where(spread_ids >= 2, 2.0, 0.0)
            + jnp.where(spread_ids >= 3, 4.0, 0.0)
        )
    ).astype(jnp.float32)


def make_features(inputs, feature_weights, phases, spread_ids):
    projected = jnp.dot(inputs, feature_weights, preferred_element_type=jnp.float32)
    return jnp.sin(projected * feature_scale(spread_ids) + phases)


def add_pair(earlier, later):
    return (earlier[0] + later[0], earlier[1] + later[1])


def gram_form(signals, targets, row_counts, feature_weights, phases, spread_ids):
    rows = signals.shape[1]
    width = feature_weights.shape[1]
    tgt_width = targets.shape[2]
    groups = lax.axis_size("asset")
    block_size = width // groups
    entries = width * tgt_width
    own_rows = row_counts[0, 0]
    all_counts = lax.all_gather(row_counts[0], "asset", axis=0, tiled=True)
    row_sum = jnp.sum(all_counts).astype(jnp.float32)
    inputs = signals[0]
    returns = targets[0]
    features = make_features(inputs, feature_weights, phases, spread_ids)
    live_mask = (jnp.arange(rows) < own_rows)[:, None]
    features = jnp.where(live_mask, features, jnp.zeros_like(features))
    returns = jnp.where(live_mask, returns.astype(jnp.float32), jnp.zeros((), jnp.float32))
    combined = jnp.concatenate([features, returns], axis=1)
    contract_rows = (((0,), (0,)), ((), ()))
    gram_block = lax.psum_scatter(
        lax.dot_general(features, combined, contract_rows, precision=lax.Precision.HIGHEST),
        "asset",
        scatter_dimension=0,
        tiled=True,
    )
    earlier, earlier_rows = prefix(
        (gram_block, row_sum),
        "epoch",
        add_pair,
        (jnp.zeros_like(gram_block), jnp.zeros((), jnp.float32)),
    )
    cumulative = earlier + gram_block
    row_total = earlier_rows + row_sum
    first_row = lax.axis_index("asset") * block_size
    diagonal = jnp.arange(width)[None, :] == first_row + jnp.arange(block_size)[:, None]
    system = cumulative[:, :width] / row_total + ridge_penalty * jnp.where(
        diagonal, 1.0, 0.0
    ).astype(jnp.float32)
    residual = cumulative[:, width:] / row_total
    coef = jnp.zeros((block_size, tgt_width), jnp.float32)
    for _ in range(ITERS):
        image = jnp.zeros((block_size, tgt_width), jnp.float32) + jnp.dot(
            system,
            lax.all_gather(residual, "asset", axis=0, tiled=True),
            precision=lax.Precision.HIGHEST,
        )
        res_norm, res_curve = lax.psum(
            (jnp.sum(residual * residual), jnp.sum(residual * image)), "asset"
        )
        step_size = res_norm / entries / (res_curve / entries + epsilon)
        coef = coef + step_size * residual
        residual = residual - step_size * image
    return (jnp.sqrt(row_total) * coef)[None]


def dot(a, b, dims):
    return lax.dot_general(a, b, dims, preferred_element_type=jnp.float32)


def split(a):
    high = a.astype(jnp.bfloat16)
    return high, (a - high.astype(jnp.float32)).astype(jnp.bfloat16)


def sine_of_turns(turns):
    fraction = turns - jnp.round(turns)
    square = fraction * fraction
    value = SINE[-1]
    for c in SINE[-2::-1]:
        value = value * square + c
    return value * fraction


def kernel_call(kernel, out_shape, in_specs, out_specs, scratch, cost=None):
    return pl.pallas_call(
        kernel,
        out_shape=out_shape,
        in_specs=in_specs,
        out_specs=out_specs,
        scratch_shapes=scratch,
        cost_estimate=cost,
        compiler_params=pltpu.CompilerParams(vmem_limit_bytes=60 * 2**20),
    )


WHOLE = pl.BlockSpec(memory_space=pltpu.VMEM)
SCALARS = pl.BlockSpec(memory_space=pltpu.SMEM)
REMOTE = pl.BlockSpec(memory_space=pl.ANY)


def rows_of(c):
    return pl.ds(pl.multiple_of(c * CHUNK, CHUNK), CHUNK)


def pack_rows(sources, rows, mark, x_buf, y_buf):
    lane = lax.broadcasted_iota(jnp.int32, (1, LANES), 1)
    counts = []
    for x_ref, y_ref, use in sources:
        for first in range(0, x_ref.shape[0], rows):
            marks = jnp.sum(y_ref[first : first + rows, :].astype(jnp.float32), axis=0, keepdims=True)
            counts.append(jnp.sum(jnp.where(lane == mark, marks, 0.0)).astype(jnp.int32) * use)
    filled = jnp.int32(0)
    count = jnp.int32(0)
    place = 0
    for x_ref, y_ref, use in sources:
        for first in range(0, x_ref.shape[0], rows):
            own = counts[place]
            place += 1
            at = pl.ds(pl.multiple_of(filled, PACK), rows)
            x_buf[at, :] = x_ref[first : first + rows, :]
            y_buf[at, :] = y_ref[first : first + rows, :]
            count = count + own
            filled = filled + (own + PACK - 1) // PACK * PACK
    end = pl.ds(pl.multiple_of(filled, PACK), CHUNK)
    x_buf[end, :] = jnp.zeros((CHUNK, x_buf.shape[1]), x_buf.dtype)
    y_buf[end, :] = jnp.zeros((CHUNK, LANES), y_buf.dtype)
    return (filled + CHUNK - 1) // CHUNK, count


def featurize_chunk(x, y, lines, w_ref, ph_ref, cross_ref, put):
    returns = y[:lines].astype(jnp.bfloat16)
    for j in range(0, w_ref.shape[1], TILE):
        js = slice(j, j + TILE)
        turns = dot(x, w_ref[:, js], NN) * TURN + ph_ref[:, js]
        high, low = split(sine_of_turns(turns))
        put(js, high, low)
        cross_ref[:, js] += dot(returns, high, NN) + dot(returns, low, NN)


def in_pairs(chunks, one):
    def pair(p, _):
        one(2 * p, 0)
        one(2 * p + 1, 1)
        return 0

    lax.fori_loop(0, chunks // 2, pair, 0)

    @pl.when(lax.rem(chunks, 2) == 1)
    def _():
        one(chunks - 1, 0)


def near_kernel(sources, rows, lines, mark, use_ref, *refs):
    x_refs, y_refs = refs[:sources], refs[sources : 2 * sources]
    w_ref, ph_ref, high_hbm, low_hbm, cross_ref, live_ref, info_ref = refs[2 * sources : 2 * sources + 7]
    x_buf, y_buf, high_buf, low_buf, high_sem, low_sem = refs[2 * sources + 7 :]
    sets = [(x_refs[s], y_refs[s], use_ref[s]) for s in range(sources)]
    chunks, count = pack_rows(sets, rows, mark, x_buf, y_buf)
    info_ref[0] = chunks
    info_ref[1] = count
    cross_ref[...] = jnp.zeros_like(cross_ref)

    def send(c, slot):
        return (
            pltpu.make_async_copy(high_buf.at[slot], high_hbm.at[rows_of(c), :], high_sem.at[slot]),
            pltpu.make_async_copy(low_buf.at[slot], low_hbm.at[rows_of(c), :], low_sem.at[slot]),
        )

    def one(c, slot):
        @pl.when(c >= 2)
        def _():
            for copy in send(c - 2, slot):
                copy.wait()

        turned = y_buf[rows_of(c), :].astype(jnp.float32).T
        live_ref[c] = turned[mark : mark + 8]

        def put(js, high, low):
            high_buf[slot, :, js] = high
            low_buf[slot, :, js] = low

        featurize_chunk(x_buf[rows_of(c), :], turned, lines, w_ref, ph_ref, cross_ref, put)
        for copy in send(c, slot):
            copy.start()

    in_pairs(chunks, one)
    for back in (2, 1):

        @pl.when(chunks >= back)
        def _():
            for copy in send(chunks - back, lax.rem(chunks - back, 2)):
                copy.wait()


def estimate(cols, r, i):
    f32 = jnp.float32
    norm = jnp.full((1, 1), jnp.sum(r[cols : cols + SHARED] * r[cols : cols + SHARED]), f32)
    curve = jnp.full((1, 1), jnp.sum(r[cols : cols + SHARED] * i[cols : cols + SHARED]), f32)
    good = jnp.logical_and(norm > 0.0, curve > ridge_penalty * 0.5 * norm)
    return jnp.where(good, norm / jnp.where(good, curve, 1.0), 1.0)


def main_kernel(sources, rows, lines, cols, mark, use_ref, info_ref, *refs):
    x_refs, y_refs = refs[:sources], refs[sources : 2 * sources]
    w_ref, ph_ref, near_cross, near_live, near_high, near_low = refs[2 * sources : 2 * sources + 6]
    v0_ref, q1_ref, q2_ref, mom_ref = refs[2 * sources + 6 : 2 * sources + 10]
    x_buf, y_buf, phi, plo, live, stack, inner, acc, v0, image, q1, high_sem, low_sem = refs[2 * sources + 10 :]
    f32, bf16 = jnp.float32, jnp.bfloat16

    near = info_ref[0]

    def begin(c, _):
        at = rows_of(c)
        pltpu.make_async_copy(near_high.at[at, :], phi.at[at, :], high_sem.at[c]).start()
        pltpu.make_async_copy(near_low.at[at, :], plo.at[at, :], low_sem.at[c]).start()
        live[c] = near_live[c]
        return 0

    lax.fori_loop(0, near, begin, 0)
    sets = [(x_refs[s], y_refs[s], use_ref[s]) for s in range(sources)]
    far, count = pack_rows(sets, rows, mark, x_buf, y_buf)
    chunks = near + far
    total = (info_ref[1] + count).astype(f32)
    inverse = 1.0 / jnp.full((1, 1), total, f32)

    v0[...] = near_cross[...]

    def featurize(c, _):
        turned = y_buf[rows_of(c), :].astype(f32).T
        live[near + c] = turned[mark : mark + 8]
        at = rows_of(near + c)

        def put(js, high, low):
            phi[at, js] = high
            plo[at, js] = low

        featurize_chunk(x_buf[rows_of(c), :], turned, lines, w_ref, ph_ref, v0, put)

    in_pairs(far, featurize)
    spans = (chunks + GROUP - 1) // GROUP

    def blank(c, _):
        phi[rows_of(c), :] = jnp.zeros((CHUNK, phi.shape[1]), bf16)
        plo[rows_of(c), :] = jnp.zeros((CHUNK, phi.shape[1]), bf16)
        live[c] = jnp.zeros(live.shape[1:], f32)
        return 0

    lax.fori_loop(chunks, spans * GROUP, blank, 0)

    def end(c, _):
        at = rows_of(c)
        pltpu.make_async_copy(near_high.at[at, :], phi.at[at, :], high_sem.at[c]).wait()
        pltpu.make_async_copy(near_low.at[at, :], plo.at[at, :], low_sem.at[c]).wait()
        return 0

    lax.fori_loop(0, near, end, 0)
    v0[...] = v0[...] * inverse

    def span_of(p):
        return pl.ds(pl.multiple_of(p * GROUP * CHUNK, GROUP * CHUNK), GROUP * CHUNK)

    def inner_of(p, part, lefts):
        half = GROUP // 2
        first = pl.multiple_of((p * 2 + part) * half * CHUNK, half * CHUNK)
        mask = jnp.concatenate([live[p * GROUP + part * half + c][0:1] for c in range(half)], axis=1)
        return dot(lefts, phi[pl.ds(first, half * CHUNK), :], NT), mask

    high, low = split(v0[...])
    stack[:lines] = high
    stack[lines:] = low
    acc[...] = jnp.zeros_like(acc)

    def first(p, _):
        for part in range(2):
            u, mask = inner_of(p, part, stack[...])
            uh, ul = split((u[:lines] + u[lines:]) * mask)
            at = slice(part * GROUP // 2 * CHUNK, (part + 1) * GROUP // 2 * CHUNK)
            inner[:lines, at] = uh
            inner[lines:, at] = ul
        acc[...] += dot(inner[...], phi[span_of(p), :], NN)
        acc[:lines] += dot(inner[:lines], plo[span_of(p), :], NN)
        return 0

    lax.fori_loop(0, spans, first, 0)
    image[...] = (acc[:lines] + acc[lines:]) * inverse + ridge_penalty * v0[...]
    shift0 = estimate(cols, v0, image)
    q1[...] = v0[...] - shift0 * image[...]
    stack[:lines] = q1[...].astype(bf16)
    acc[:lines] = jnp.zeros((lines, acc.shape[1]), f32)

    def second(p, _):
        for part in range(2):
            u, mask = inner_of(p, part, stack[:lines])
            at = slice(part * GROUP // 2 * CHUNK, (part + 1) * GROUP // 2 * CHUNK)
            inner[:lines, at] = (u * mask).astype(bf16)
        acc[:lines] += dot(inner[:lines], phi[span_of(p), :], NN)
        return 0

    lax.fori_loop(0, spans, second, 0)
    acc[:lines] = acc[:lines] * inverse + ridge_penalty * q1[...]
    shift1 = estimate(cols, q1, acc)
    v0_ref[...] = v0[:cols]
    q1_ref[...] = q1[:cols]
    q2_ref[...] = q1[:cols] - shift1 * acc[:cols]
    stack[:cols] = q2_ref[...].astype(bf16)

    def curve(p, total_sq):
        for part in range(2):
            u, mask = inner_of(p, part, stack[:cols])
            total_sq = total_sq + jnp.square(u * mask)
        return total_sq

    squares = lax.fori_loop(0, spans, curve, jnp.zeros((cols, GROUP // 2 * CHUNK), f32))
    vectors = (v0_ref, q1_ref, q2_ref)
    images = (image, acc)
    pairs = [jnp.sum(vectors[i][...] * vectors[j][...]) for i in range(3) for j in range(i, 3)]
    pairs += [jnp.sum(vectors[i][...] * images[j][:cols]) for j in range(2) for i in range(j, 3)]
    pairs.append(jnp.sum(squares) / total + ridge_penalty * pairs[5])
    for i, m in enumerate(pairs):
        mom_ref[i] = m
    mom_ref[12] = jnp.sum(shift0)
    mom_ref[13] = jnp.sum(shift1)
    mom_ref[14] = total
    mom_ref[15] = total


def finish_kernel(groups, entries, *refs):
    share_refs = refs[:groups]
    mom_ref = share_refs[0]
    v0_ref, q1_ref, q2_ref, out_ref = refs[groups:]
    f32 = jnp.float32

    def local(i):
        return jnp.full((1, LANES), mom_ref[i], f32)

    def mean(i):
        return jnp.full((1, LANES), sum(ref[i] for ref in share_refs), f32) / entries

    g = {}
    for n, (i, j) in enumerate(((0, 0), (0, 1), (0, 2), (1, 1), (1, 2), (2, 2))):
        g[i, j] = g[j, i] = mean(n)
    h = {}
    for n, (i, j) in enumerate(((0, 0), (1, 0), (2, 0), (1, 1), (2, 1), (2, 2))):
        h[i, j] = h[j, i] = mean(6 + n)
    shift0, shift1, total = local(12), local(13), local(14)

    def form(table, r):
        return sum(r[i] * r[j] * table[i, j] for i in range(3) for j in range(3))

    def step_of(r):
        return jnp.clip(form(g, r) / (form(h, r) + epsilon), 0.0, 1.0 / ridge_penalty)

    one = jnp.ones((1, LANES), f32)
    zero = jnp.zeros((1, LANES), f32)
    r0 = (one, zero, zero)
    step0 = g[0, 0] / (h[0, 0] + epsilon)
    ratio = step0 / shift0
    r1 = (one - ratio, ratio, zero)
    step1 = step_of(r1)
    left, right = r1[0] / shift0, r1[1] / shift1
    r2 = (r1[0] - step1 * left, r1[1] - step1 * (right - left), step1 * right)
    step2 = step_of(r2)
    root = jnp.sqrt(total)
    k = [(root * (step0 * r0[i] + step1 * r1[i] + step2 * r2[i]))[:, :1] for i in range(3)]
    piece = v0_ref.shape[1] // groups
    for owner in range(groups):
        at = slice(owner * piece, (owner + 1) * piece)
        out_ref[owner] = k[0] * v0_ref[:, at] + k[1] * q1_ref[:, at] + k[2] * q2_ref[:, at]


def factor_form(signals, targets, row_counts, feature_weights, phases, spread_ids):
    _, rows, depth = signals.shape
    width = feature_weights.shape[1]
    tgt_width = targets.shape[2]
    groups = lax.axis_size("asset")
    epochs = lax.axis_size("epoch")
    cols = tgt_width // groups
    mark = cols + SHARED
    lines = (mark + 1 + SUBLANES - 1) // SUBLANES * SUBLANES
    piece = width // groups
    f32, bf16 = jnp.float32, jnp.bfloat16
    asset = lax.axis_index("asset")
    epoch = lax.axis_index("epoch")

    def rotate(a, s):
        return lax.ppermute(a, "asset", [(i, (i + s) % groups) for i in range(groups)])

    def swap(a, bit):
        return lax.ppermute(a, "epoch", [(e, e ^ bit) for e in range(epochs)])

    x = signals[0]
    x_own = [x] + [rotate(x, s) for s in range(1, groups)]
    alive = (jnp.arange(rows) < row_counts[0, 0])[:, None]
    returns = jnp.where(alive, targets[0], jnp.zeros((), bf16))
    rest = jnp.concatenate(
        [returns[:, :SHARED], alive.astype(bf16), jnp.zeros((rows, LANES - mark - 1), bf16)], axis=1
    )
    payload = jnp.stack(
        [
            jnp.concatenate([returns[:, g * cols : (g + 1) * cols], rest], axis=1)
            for g in range(groups)
        ]
    )
    y_own = []
    for s in range(groups):
        mine = lax.dynamic_index_in_dim(payload, (asset + s) % groups, 0, False)
        y_own.append(rotate(mine, s) if s else mine)
    y_own = jnp.concatenate(y_own)
    held = [(x_own, y_own, 0)]
    bit = epochs // 2
    while bit > 1:
        more = []
        for xs, y, o in held:
            more.append(([swap(b, bit) for b in xs], swap(y, bit), o ^ bit))
        held = held + more
        bit //= 2
    held = [(jnp.concatenate(xs), y, o) for xs, y, o in held]
    held = held + [(swap(xs, 1), swap(y, 1), o ^ 1) for xs, y, o in held]
    near = [h for h in held if h[2] == 0]
    far = [h for h in held if h[2] != 0]

    def used(sources):
        return jnp.stack([((epoch ^ o) <= epoch).astype(jnp.int32) for _, _, o in sources])

    scaled = (feature_weights.astype(f32) * feature_scale(spread_ids)).astype(bf16)
    offsets = (phases * TURN)[None, :]

    def shape(*dims, dtype=f32):
        return jax.ShapeDtypeStruct(dims, dtype)

    span = groups * rows
    limit = len(near) * span
    high, low, cross, live, info = kernel_call(
        lambda *refs: near_kernel(len(near), rows, lines, mark, *refs),
        (
            shape(limit, width, dtype=bf16),
            shape(limit, width, dtype=bf16),
            shape(lines, width),
            shape(limit // CHUNK, 8, CHUNK),
            shape(2, dtype=jnp.int32),
        ),
        [SCALARS] + [WHOLE] * (2 * len(near) + 2),
        (REMOTE, REMOTE, WHOLE, WHOLE, SCALARS),
        [
            pltpu.VMEM((limit + CHUNK, depth), bf16),
            pltpu.VMEM((limit + CHUNK, LANES), bf16),
            pltpu.VMEM((2, CHUNK, width), bf16),
            pltpu.VMEM((2, CHUNK, width), bf16),
            pltpu.SemaphoreType.DMA((2,)),
            pltpu.SemaphoreType.DMA((2,)),
        ],
        pl.CostEstimate(flops=10**10, transcendentals=limit * width, bytes_accessed=5 * 10**7),
    )(used(near), *[a for a, _, _ in near], *[y for _, y, _ in near], scaled, offsets)

    limit = len(far) * span
    whole = len(held) * span
    vector = shape(cols, width)
    v0, q1, q2, moments = kernel_call(
        lambda *refs: main_kernel(len(far), rows, lines, cols, mark, *refs),
        (vector, vector, vector, shape(16)),
        [SCALARS] * 2 + [WHOLE] * (2 * len(far) + 4) + [REMOTE] * 2,
        (WHOLE, WHOLE, WHOLE, SCALARS),
        [
            pltpu.VMEM((limit + CHUNK, depth), bf16),
            pltpu.VMEM((limit + CHUNK, LANES), bf16),
            pltpu.VMEM((whole, width), bf16),
            pltpu.VMEM((whole, width), bf16),
            pltpu.VMEM((whole // CHUNK, 8, CHUNK), f32),
            pltpu.VMEM((2 * lines, width), bf16),
            pltpu.VMEM((2 * lines, GROUP * CHUNK), bf16),
            pltpu.VMEM((2 * lines, width), f32),
            pltpu.VMEM((lines, width), f32),
            pltpu.VMEM((lines, width), f32),
            pltpu.VMEM((lines, width), f32),
            pltpu.SemaphoreType.DMA((len(near) * span // CHUNK,)),
            pltpu.SemaphoreType.DMA((len(near) * span // CHUNK,)),
        ],
    )(
        used(far), info, *[a for a, _, _ in far], *[y for _, y, _ in far],
        scaled, offsets, cross, live, high, low,
    )
    shares = [rotate(moments, s) if s else moments for s in range(groups)]
    coef = kernel_call(
        lambda *refs: finish_kernel(groups, width * tgt_width, *refs),
        shape(groups, cols, piece),
        [SCALARS] * groups + [WHOLE] * 3,
        WHOLE,
        [],
    )(*shares, v0, q1, q2)
    coef = lax.all_to_all(coef, "asset", 0, 0, tiled=True)
    return coef.reshape(tgt_width, piece).T[None]


def on_device(signals, targets, row_counts, feature_weights, phases, spread_ids):
    epochs = lax.axis_size("epoch")
    groups = lax.axis_size("asset")
    width = feature_weights.shape[1]
    rows = signals.shape[1]
    cols = targets.shape[2] // groups
    fits = (
        epochs * groups * rows <= 2 * width
        and epochs & (epochs - 1) == 0
        and epochs >= 4
        and rows % CHUNK == 0
        and epochs * groups * rows % (GROUP * CHUNK) == 0
        and width % TILE == 0
        and cols % 8 == 0
        and (width // groups) % LANES == 0
        and cols + SHARED + 8 <= LANES
    )
    form = factor_form if fits else gram_form
    return form(signals, targets, row_counts, feature_weights, phases, spread_ids)


def solution(mesh):
    placed = (
        P(("grp", "epoch"), "asset", None),
        P(("grp", "epoch"), "asset", None),
        P(("grp", "epoch"), "asset"),
        P(),
        P(),
        P(),
    )
    return jax.shard_map(
        on_device,
        mesh=mesh,
        in_specs=placed,
        out_specs=P(("grp", "epoch"), "asset", None),
        check_vma=False,
    )
```

```python
import jax
import jax.numpy as jnp
from jax import lax
from jax.experimental import pallas as pl
from jax.experimental.pallas import tpu as pltpu
from jax.sharding import PartitionSpec as P


ITERS = 3


ridge_penalty = 0.05
epsilon = 1e-06

CHUNK = 256
HALF = 512
TILE = 256
PACK = 16
SHARED = 8
SUBLANES = 16
LANES = 128
TURN = 0.15915494309189535
SINE = (
    6.283182818537488,
    -41.34142139758713,
    81.59618384799899,
    -76.58010029406394,
    41.20539392705353,
    -12.27126097383172,
)
NT = (((1,), (1,)), ((), ()))
NN = (((1,), (0,)), ((), ()))


def prefix(part, axis, combine, identity):
    place = lax.axis_index(axis)
    gathered = jax.tree.map(lambda a: lax.all_gather(a, axis), part)
    state = jax.tree.map(lambda a, e: jnp.zeros_like(a) + jnp.asarray(e, a.dtype), part, identity)

    def one(hop, state):
        return combine(
            state, jax.tree.map(lambda a: lax.dynamic_index_in_dim(a, hop, 0, False), gathered)
        )

    return lax.fori_loop(0, place, one, state)


def feature_scale(spread_ids):
    return (
        0.5
        * (
            1.0
            + jnp.where(spread_ids >= 1, 1.0, 0.0)
            + jnp.where(spread_ids >= 2, 2.0, 0.0)
            + jnp.where(spread_ids >= 3, 4.0, 0.0)
        )
    ).astype(jnp.float32)


def make_features(inputs, feature_weights, phases, spread_ids):
    projected = jnp.dot(inputs, feature_weights, preferred_element_type=jnp.float32)
    return jnp.sin(projected * feature_scale(spread_ids) + phases)


def add_pair(earlier, later):
    return (earlier[0] + later[0], earlier[1] + later[1])


def gram_form(signals, targets, row_counts, feature_weights, phases, spread_ids):
    rows = signals.shape[1]
    width = feature_weights.shape[1]
    tgt_width = targets.shape[2]
    groups = lax.axis_size("asset")
    block_size = width // groups
    entries = width * tgt_width
    own_rows = row_counts[0, 0]
    all_counts = lax.all_gather(row_counts[0], "asset", axis=0, tiled=True)
    row_sum = jnp.sum(all_counts).astype(jnp.float32)
    inputs = signals[0]
    returns = targets[0]
    features = make_features(inputs, feature_weights, phases, spread_ids)
    live_mask = (jnp.arange(rows) < own_rows)[:, None]
    features = jnp.where(live_mask, features, jnp.zeros_like(features))
    returns = jnp.where(live_mask, returns.astype(jnp.float32), jnp.zeros((), jnp.float32))
    combined = jnp.concatenate([features, returns], axis=1)
    contract_rows = (((0,), (0,)), ((), ()))
    gram_block = lax.psum_scatter(
        lax.dot_general(features, combined, contract_rows, precision=lax.Precision.HIGHEST),
        "asset",
        scatter_dimension=0,
        tiled=True,
    )
    earlier, earlier_rows = prefix(
        (gram_block, row_sum),
        "epoch",
        add_pair,
        (jnp.zeros_like(gram_block), jnp.zeros((), jnp.float32)),
    )
    cumulative = earlier + gram_block
    row_total = earlier_rows + row_sum
    first_row = lax.axis_index("asset") * block_size
    diagonal = jnp.arange(width)[None, :] == first_row + jnp.arange(block_size)[:, None]
    system = cumulative[:, :width] / row_total + ridge_penalty * jnp.where(
        diagonal, 1.0, 0.0
    ).astype(jnp.float32)
    residual = cumulative[:, width:] / row_total
    coef = jnp.zeros((block_size, tgt_width), jnp.float32)
    for _ in range(ITERS):
        image = jnp.zeros((block_size, tgt_width), jnp.float32) + jnp.dot(
            system,
            lax.all_gather(residual, "asset", axis=0, tiled=True),
            precision=lax.Precision.HIGHEST,
        )
        res_norm, res_curve = lax.psum(
            (jnp.sum(residual * residual), jnp.sum(residual * image)), "asset"
        )
        step_size = res_norm / entries / (res_curve / entries + epsilon)
        coef = coef + step_size * residual
        residual = residual - step_size * image
    return (jnp.sqrt(row_total) * coef)[None]


def dot(a, b, dims):
    return lax.dot_general(a, b, dims, preferred_element_type=jnp.float32)


def split(a):
    high = a.astype(jnp.bfloat16)
    return high, (a - high.astype(jnp.float32)).astype(jnp.bfloat16)


def sine_of_turns(turns):
    fraction = turns - jnp.round(turns)
    square = fraction * fraction
    value = SINE[-1]
    for c in SINE[-2::-1]:
        value = value * square + c
    return value * fraction


def kernel_call(kernel, out_shape, in_specs, out_specs, scratch, cost=None):
    return pl.pallas_call(
        kernel,
        out_shape=out_shape,
        in_specs=in_specs,
        out_specs=out_specs,
        scratch_shapes=scratch,
        cost_estimate=cost,
        compiler_params=pltpu.CompilerParams(vmem_limit_bytes=60 * 2**20),
    )


WHOLE = pl.BlockSpec(memory_space=pltpu.VMEM)
SCALARS = pl.BlockSpec(memory_space=pltpu.SMEM)
REMOTE = pl.BlockSpec(memory_space=pl.ANY)


def rows_of(c):
    return pl.ds(pl.multiple_of(c * CHUNK, CHUNK), CHUNK)


def featurize_block(x, w_ref, ph_ref, put):
    for j in range(0, w_ref.shape[1], TILE):
        js = slice(j, j + TILE)
        turns = dot(x, w_ref[:, js], NN) * TURN + ph_ref[:, js]
        put(js, *split(sine_of_turns(turns)))


def near_kernel(blocks, *refs):
    x_refs = refs[:blocks]
    y_ref, w_ref, ph_ref, high_hbm, low_hbm, cross_ref, high_buf, low_buf, high_sem, low_sem = refs[blocks:]
    rows = x_refs[0].shape[0]
    lines = cross_ref.shape[0]
    cross_ref[...] = jnp.zeros_like(cross_ref)
    copies = []
    for b, x_ref in enumerate(x_refs):
        at = slice(b * rows, (b + 1) * rows)

        returns = y_ref[at, :].astype(jnp.float32).T[:lines].astype(jnp.bfloat16)

        def put(js, high, low, b=b, returns=returns):
            high_buf[b, :, js] = high
            low_buf[b, :, js] = low
            cross_ref[:, js] += dot(returns, high, NN) + dot(returns, low, NN)

        featurize_block(x_ref[...], w_ref, ph_ref, put)
        copies += [
            pltpu.make_async_copy(high_buf.at[b], high_hbm.at[at, :], high_sem.at[b]),
            pltpu.make_async_copy(low_buf.at[b], low_hbm.at[at, :], low_sem.at[b]),
        ]
        for copy in copies[-2:]:
            copy.start()
    for copy in copies:
        copy.wait()


def in_pairs(chunks, one):
    def pair(p, _):
        one(2 * p)
        one(2 * p + 1)
        return 0

    lax.fori_loop(0, chunks // 2, pair, 0)

    @pl.when(lax.rem(chunks, 2) == 1)
    def _():
        one(chunks - 1)


def in_halves(halves, body):
    def four(p, _):
        body(4 * p, 4)
        return 0

    lax.fori_loop(0, halves // 4, four, 0)

    @pl.when(lax.rem(halves, 4) >= 2)
    def _():
        body(halves // 4 * 4, 2)

    @pl.when(lax.rem(halves, 2) == 1)
    def _():
        body(halves - 1, 1)


def estimate(cols, r, i):
    f32 = jnp.float32
    norm = jnp.full((1, 1), jnp.sum(r[cols : cols + SHARED] * r[cols : cols + SHARED]), f32)
    curve = jnp.full((1, 1), jnp.sum(r[cols : cols + SHARED] * i[cols : cols + SHARED]), f32)
    good = jnp.logical_and(norm > 0.0, curve > ridge_penalty * 0.5 * norm)
    return jnp.where(good, norm / jnp.where(good, curve, 1.0), 1.0)


def main_kernel(sources, rows, lines, cols, mark, use_ref, *refs):
    x_refs, y_refs = refs[:sources], refs[sources : 2 * sources]
    near_y, w_ref, ph_ref, near_cross, near_high, near_low = refs[2 * sources : 2 * sources + 6]
    v0_ref, q1_ref, q2_ref, mom_ref = refs[2 * sources + 6 : 2 * sources + 10]
    x_buf, y_buf, phi, plo, live, stack, inner, acc, v0, image, q1, squares, sems = refs[2 * sources + 10 :]
    f32, bf16 = jnp.float32, jnp.bfloat16
    lane = lax.broadcasted_iota(jnp.int32, (1, LANES), 1)

    def count_of(y_ref, first):
        marks = jnp.sum(y_ref[first : first + rows, :].astype(f32), axis=0, keepdims=True)
        return jnp.sum(jnp.where(lane == mark, marks, 0.0)).astype(jnp.int32)

    span = near_y.shape[0]
    blocks = span // rows
    counts = [count_of(near_y, b * rows) for b in range(blocks)]
    counts += [count_of(y_refs[s], b * rows) * use_ref[s] for s in range(sources) for b in range(blocks)]
    filled = jnp.int32(0)
    places = []
    for own in counts:
        places.append((filled, own))
        filled = filled + (own + PACK - 1) // PACK * PACK
    total = sum(own for _, own in places).astype(f32)
    inverse = 1.0 / jnp.full((1, 1), total, f32)
    far_from = places[blocks][0]
    far_chunks = (filled - far_from + CHUNK - 1) // CHUNK
    halves = (filled + HALF - 1) // HALF

    def landing(then):
        for b in range(blocks):
            first, own = places[b]
            packs = (own + PACK - 1) // PACK
            size, digit = rows, 0
            while size >= PACK:
                done = packs * PACK // (2 * size) * (2 * size)

                @pl.when(lax.rem(packs * PACK // size, 2) == 1)
                def _(b=b, first=first, size=size, digit=digit, done=done):
                    source = pl.ds(pl.multiple_of(b * rows + done, PACK), size)
                    target = pl.ds(pl.multiple_of(first + done, PACK), size)
                    for k, (hbm, buf) in enumerate(((near_high, phi), (near_low, plo))):
                        then(pltpu.make_async_copy(hbm.at[source, :], buf.at[target, :], sems.at[k, b, digit]))

                size //= 2
                digit += 1

    landing(lambda copy: copy.start())
    for i in range(blocks, len(places)):
        s, first = (i - blocks) // blocks, (i - blocks) % blocks * rows
        at = pl.ds(pl.multiple_of(places[i][0] - far_from, PACK), rows)
        x_buf[at, :] = x_refs[s][first : first + rows, :]
        y_buf[at, :] = y_refs[s][first : first + rows, :]
    end = pl.ds(pl.multiple_of(filled - far_from, PACK), CHUNK)
    x_buf[end, :] = jnp.zeros((CHUNK, x_buf.shape[1]), bf16)
    y_buf[end, :] = jnp.zeros((CHUNK, LANES), bf16)

    def mark_live(h, _):
        slot = lax.broadcasted_iota(jnp.int32, (1, HALF), 1) + h * HALF
        alive = jnp.zeros((1, HALF), f32)
        for first, own in places:
            alive = jnp.where(jnp.logical_and(slot >= first, slot < first + own), 1.0, alive)
        live[h, 0:1] = alive
        return 0

    lax.fori_loop(0, halves, mark_live, 0)

    v0[...] = near_cross[...]

    def featurize(c):
        at = rows_of(c)
        to = pl.ds(pl.multiple_of(far_from + c * CHUNK, PACK), CHUNK)
        returns = y_buf[at, :].astype(f32).T[:lines].astype(bf16)

        def put(js, high, low):
            phi[to, js] = high
            plo[to, js] = low
            v0[:, js] += dot(returns, high, NN) + dot(returns, low, NN)

        featurize_block(x_buf[at, :], w_ref, ph_ref, put)

    in_pairs(far_chunks, featurize)
    end = pl.ds(pl.multiple_of(filled, PACK), HALF)
    phi[end, :] = jnp.zeros((HALF, phi.shape[1]), bf16)
    plo[end, :] = jnp.zeros((HALF, phi.shape[1]), bf16)
    landing(lambda copy: copy.wait())
    v0[...] = v0[...] * inverse

    def rows_from(h, n):
        return pl.ds(pl.multiple_of(h * HALF, HALF), n * HALF)

    high, low = split(v0[...])
    stack[:lines] = high
    stack[lines:] = low
    acc[...] = jnp.zeros_like(acc)

    def first(h, n):
        for i in range(n):
            u = dot(stack[...], phi[rows_from(h + i, 1), :], NT)
            uh, ul = split((u[:lines] + u[lines:]) * live[h + i, 0:1])
            inner[:lines, i * HALF : (i + 1) * HALF] = uh
            inner[lines:, i * HALF : (i + 1) * HALF] = ul
        acc[...] += dot(inner[:, : n * HALF], phi[rows_from(h, n), :], NN)
        acc[:lines] += dot(inner[:lines, : n * HALF], plo[rows_from(h, n), :], NN)

    in_halves(halves, first)
    image[...] = (acc[:lines] + acc[lines:]) * inverse + ridge_penalty * v0[...]
    shift0 = estimate(cols, v0, image)
    q1[...] = v0[...] - shift0 * image[...]
    stack[:lines] = q1[...].astype(bf16)
    acc[:lines] = jnp.zeros((lines, acc.shape[1]), f32)

    def second(h, n):
        for i in range(n):
            u = dot(stack[:lines], phi[rows_from(h + i, 1), :], NT) * live[h + i, 0:1]
            inner[:lines, i * HALF : (i + 1) * HALF] = u.astype(bf16)
        acc[:lines] += dot(inner[:lines, : n * HALF], phi[rows_from(h, n), :], NN)

    in_halves(halves, second)
    acc[:lines] = acc[:lines] * inverse + ridge_penalty * q1[...]
    shift1 = estimate(cols, q1, acc)
    v0_ref[...] = v0[:cols]
    q1_ref[...] = q1[:cols]
    q2_ref[...] = q1[:cols] - shift1 * acc[:cols]
    stack[:cols] = q2_ref[...].astype(bf16)
    squares[...] = jnp.zeros_like(squares)

    def curve(h, n):
        part = jnp.zeros((cols, HALF), f32)
        for i in range(n):
            part += jnp.square(dot(stack[:cols], phi[rows_from(h + i, 1), :], NT) * live[h + i, 0:1])
        squares[...] += part

    in_halves(halves, curve)
    vectors = (v0_ref, q1_ref, q2_ref)
    images = (image, acc)
    pairs = [jnp.sum(vectors[i][...] * vectors[j][...]) for i in range(3) for j in range(i, 3)]
    pairs += [jnp.sum(vectors[i][...] * images[j][:cols]) for j in range(2) for i in range(j, 3)]
    pairs.append(jnp.sum(squares[...]) / total + ridge_penalty * pairs[5])
    for i, m in enumerate(pairs):
        mom_ref[i] = m
    mom_ref[12] = jnp.sum(shift0)
    mom_ref[13] = jnp.sum(shift1)
    mom_ref[14] = total
    mom_ref[15] = total


def finish_kernel(groups, entries, *refs):
    share_refs = refs[:groups]
    mom_ref = share_refs[0]
    v0_ref, q1_ref, q2_ref, out_ref = refs[groups:]
    f32 = jnp.float32

    def local(i):
        return jnp.full((1, LANES), mom_ref[i], f32)

    def mean(i):
        return jnp.full((1, LANES), sum(ref[i] for ref in share_refs), f32) / entries

    g = {}
    for n, (i, j) in enumerate(((0, 0), (0, 1), (0, 2), (1, 1), (1, 2), (2, 2))):
        g[i, j] = g[j, i] = mean(n)
    h = {}
    for n, (i, j) in enumerate(((0, 0), (1, 0), (2, 0), (1, 1), (2, 1), (2, 2))):
        h[i, j] = h[j, i] = mean(6 + n)
    shift0, shift1, total = local(12), local(13), local(14)

    def form(table, r):
        return sum(r[i] * r[j] * table[i, j] for i in range(3) for j in range(3))

    def step_of(r):
        return jnp.clip(form(g, r) / (form(h, r) + epsilon), 0.0, 1.0 / ridge_penalty)

    one = jnp.ones((1, LANES), f32)
    zero = jnp.zeros((1, LANES), f32)
    r0 = (one, zero, zero)
    step0 = g[0, 0] / (h[0, 0] + epsilon)
    ratio = step0 / shift0
    r1 = (one - ratio, ratio, zero)
    step1 = step_of(r1)
    left, right = r1[0] / shift0, r1[1] / shift1
    r2 = (r1[0] - step1 * left, r1[1] - step1 * (right - left), step1 * right)
    step2 = step_of(r2)
    root = jnp.sqrt(total)
    k = [(root * (step0 * r0[i] + step1 * r1[i] + step2 * r2[i]))[:, :1] for i in range(3)]
    piece = v0_ref.shape[1] // groups
    for owner in range(groups):
        at = slice(owner * piece, (owner + 1) * piece)
        out_ref[owner] = k[0] * v0_ref[:, at] + k[1] * q1_ref[:, at] + k[2] * q2_ref[:, at]


def factor_form(signals, targets, row_counts, feature_weights, phases, spread_ids):
    _, rows, depth = signals.shape
    width = feature_weights.shape[1]
    tgt_width = targets.shape[2]
    groups = lax.axis_size("asset")
    epochs = lax.axis_size("epoch")
    cols = tgt_width // groups
    mark = cols + SHARED
    lines = (mark + 1 + SUBLANES - 1) // SUBLANES * SUBLANES
    piece = width // groups
    f32, bf16 = jnp.float32, jnp.bfloat16
    asset = lax.axis_index("asset")
    epoch = lax.axis_index("epoch")

    def rotate(a, s):
        return lax.ppermute(a, "asset", [(i, (i + s) % groups) for i in range(groups)])

    def swap(a, bit):
        return lax.ppermute(a, "epoch", [(e, e ^ bit) for e in range(epochs)])

    x = signals[0]
    x_own = [x] + [rotate(x, s) for s in range(1, groups)]
    alive = (jnp.arange(rows) < row_counts[0, 0])[:, None]
    returns = jnp.where(alive, targets[0], jnp.zeros((), bf16))
    rest = jnp.concatenate(
        [returns[:, :SHARED], alive.astype(bf16), jnp.zeros((rows, LANES - mark - 1), bf16)], axis=1
    )
    payload = jnp.stack(
        [
            jnp.concatenate([returns[:, g * cols : (g + 1) * cols], rest], axis=1)
            for g in range(groups)
        ]
    )
    y_own = []
    for s in range(groups):
        mine = lax.dynamic_index_in_dim(payload, (asset + s) % groups, 0, False)
        y_own.append(rotate(mine, s) if s else mine)
    y_own = jnp.concatenate(y_own)
    x_held, y_held = [(x_own, 0)], [(y_own, 0)]
    bit = epochs // 2
    while bit > 1:
        x_held = x_held + [([swap(b, bit) for b in xs], o ^ bit) for xs, o in x_held]
        y_held = y_held + [(swap(y, bit), o ^ bit) for y, o in y_held]
        bit //= 2
    x_all = jnp.concatenate(x_own)
    x_held = [(x_all, 0)] + [(jnp.concatenate(xs), o) for xs, o in x_held[1:]]
    x_far = [(swap(x_held[0][0], 1), 1)]
    y_far = [(swap(y_own, 1), 1)]
    x_far += x_held[1:] + [(swap(xs, 1), o ^ 1) for xs, o in x_held[1:]]
    y_far += y_held[1:] + [(swap(y, 1), o ^ 1) for y, o in y_held[1:]]
    use = jnp.stack([((epoch ^ o) <= epoch).astype(jnp.int32) for _, o in x_far])

    scaled = (feature_weights.astype(f32) * feature_scale(spread_ids)).astype(bf16)
    offsets = (phases * TURN)[None, :]

    def shape(*dims, dtype=f32):
        return jax.ShapeDtypeStruct(dims, dtype)

    span = groups * rows
    high, low, cross = kernel_call(
        lambda *refs: near_kernel(groups, *refs),
        (shape(span, width, dtype=bf16),) * 2 + (shape(lines, width),),
        [WHOLE] * (groups + 3),
        (REMOTE, REMOTE, WHOLE),
        [
            pltpu.VMEM((groups, rows, width), bf16),
            pltpu.VMEM((groups, rows, width), bf16),
            pltpu.SemaphoreType.DMA((groups,)),
            pltpu.SemaphoreType.DMA((groups,)),
        ],
    )(*x_own, y_own, scaled, offsets)

    limit = len(x_far) * span
    whole = limit + span
    vector = shape(cols, width)
    v0, q1, q2, moments = kernel_call(
        lambda *refs: main_kernel(len(x_far), rows, lines, cols, mark, *refs),
        (vector, vector, vector, shape(16)),
        [SCALARS] + [WHOLE] * (2 * len(x_far) + 4) + [REMOTE] * 2,
        (WHOLE, WHOLE, WHOLE, SCALARS),
        [
            pltpu.VMEM((limit + CHUNK, depth), bf16),
            pltpu.VMEM((limit + CHUNK, LANES), bf16),
            pltpu.VMEM((whole + HALF, width), bf16),
            pltpu.VMEM((whole + HALF, width), bf16),
            pltpu.VMEM((whole // HALF, 8, HALF), f32),
            pltpu.VMEM((2 * lines, width), bf16),
            pltpu.VMEM((2 * lines, 4 * HALF), bf16),
            pltpu.VMEM((2 * lines, width), f32),
            pltpu.VMEM((lines, width), f32),
            pltpu.VMEM((lines, width), f32),
            pltpu.VMEM((lines, width), f32),
            pltpu.VMEM((cols, HALF), f32),
            pltpu.SemaphoreType.DMA((2, groups, (rows // PACK).bit_length())),
        ],
    )(use, *[xs for xs, _ in x_far], *[y for y, _ in y_far], y_own, scaled, offsets, cross, high, low)
    shares = [rotate(moments, s) if s else moments for s in range(groups)]
    coef = kernel_call(
        lambda *refs: finish_kernel(groups, width * tgt_width, *refs),
        shape(groups, cols, piece),
        [SCALARS] * groups + [WHOLE] * 3,
        WHOLE,
        [],
    )(*shares, v0, q1, q2)
    coef = lax.all_to_all(coef, "asset", 0, 0, tiled=True)
    return coef.reshape(tgt_width, piece).T[None]


def on_device(signals, targets, row_counts, feature_weights, phases, spread_ids):
    epochs = lax.axis_size("epoch")
    groups = lax.axis_size("asset")
    width = feature_weights.shape[1]
    rows = signals.shape[1]
    cols = targets.shape[2] // groups
    fits = (
        epochs * groups * rows <= 2 * width
        and epochs & (epochs - 1) == 0
        and epochs >= 2
        and rows % CHUNK == 0
        and rows & (rows - 1) == 0
        and epochs * groups * rows % HALF == 0
        and width % TILE == 0
        and cols % 8 == 0
        and (width // groups) % LANES == 0
        and cols + SHARED + 8 <= LANES
    )
    form = factor_form if fits else gram_form
    return form(signals, targets, row_counts, feature_weights, phases, spread_ids)


def solution(mesh):
    placed = (
        P(("grp", "epoch"), "asset", None),
        P(("grp", "epoch"), "asset", None),
        P(("grp", "epoch"), "asset"),
        P(),
        P(),
        P(),
    )
    return jax.shard_map(
        on_device,
        mesh=mesh,
        in_specs=placed,
        out_specs=P(("grp", "epoch"), "asset", None),
        check_vma=False,
    )
```
